32 devices in a mesh: pair: 4 (over x, core), row: 2 (over y), col: 4 (over z).
Axes of the slice: x: 2, y: 2, z: 4, core: 2. Of those that a mesh axis runs over, the one named last changes fastest.
Arguments:
- coords: float32 [4, 30, 512], P('pair', None, ('row', 'col')), may hold values from -1.6 to 1.6
- final_coords: float32 [30, 512], P(None, ('row', 'col')), may hold values from -1.6 to 1.6
- growth: float32 [4, 512], P('pair', ('row', 'col')), may hold values from 0.4 to 2.5
- counts: int32 [5], replicated, may hold values from 256 to 512, as said below
- labels: int32 [512], P(('row', 'col')), may hold values from 0 to 15
Outputs:
- fates: float32 [4, 16, 512], P('pair', None, ('row', 'col'))
- mass: float32 [4, 512], P('pair', ('row', 'col'))
The draws below stay inside these ranges and needn't reach their ends.
Inputs may be any that keep to these rules, and one draw needn't show every extreme that they name: The cells of a timepoint are its first counts positions; some timepoint has all 512.
All inputs are finite; a program needn't handle non-finite values.
Results may differ from the reference program's by a relative error of at most 0.0001.
Values sent between devices are 32-bit elements; how exact they have to be, the bound alone decides.
A program may use at most 64 MiB of HBM per device.

```python
import math
import jax
import jax.numpy as jnp
from jax import lax

PCA = 30
CLASSES = 16
PAIRS = 4
CELLS = 512


def membership(key, moment):
    member_key = jax.random.fold_in(jax.random.fold_in(key, 51), moment)
    return jax.random.randint(member_key, (CELLS,), 0, CLASSES).astype(jnp.int32)


def cloud(key, moment):
    member = membership(key, moment)
    across = (member % 4).astype(jnp.float32) * 0.9 - 1.35
    downward = (member // 4).astype(jnp.float32) * 0.9 - 1.35
    noise_key = jax.random.fold_in(jax.random.fold_in(key, 52), moment)
    near_noise = 0.12 * jax.random.normal(jax.random.fold_in(noise_key, 3), (2, CELLS), jnp.float32)
    far_noise = 0.3 * jax.random.normal(jax.random.fold_in(noise_key, 4), (PCA - 2, CELLS), jnp.float32)
    centers = jnp.stack([across, downward], axis=0)
    values = jnp.concatenate([centers + near_noise, far_noise], axis=0)
    return jnp.clip(values, -1.6, 1.6).astype(jnp.float32)


def draw_coords(key, part):
    return jnp.stack([cloud(key, moment) for moment in range(PAIRS)], axis=0)


def draw_final_coords(key, part):
    return cloud(key, PAIRS)


def draw_labels(key, part):
    return membership(key, PAIRS)


def draw_counts(key, part):
    base = jax.random.randint(jax.random.fold_in(key, 41), (PAIRS + 1,), CELLS // 2, CELLS + 1)
    chosen = jax.random.randint(jax.random.fold_in(key, 42), (), 0, PAIRS + 1)
    return jnp.where(jnp.arange(PAIRS + 1) == chosen, CELLS, base).astype(jnp.int32)


def block_levels(rng, dims, split, least, top_value):
    def one(dim, shards_of):
        heights = jax.random.uniform(jax.random.fold_in(jax.random.fold_in(rng, 6), dim), (shards_of,), jnp.float32, least / len(split), top_value / len(split))
        return jnp.repeat(jnp.exp(heights), dims[dim] // shards_of).reshape((-1,) + (1,) * (len(dims) - dim - 1))

    factor_of = one(*split[0])
    for cut in split[1:]:
        factor_of = factor_of * one(*cut)
    return factor_of


def setup_inputs(seed: int = 0) -> dict:
    seeds = jax.random.split(jax.random.key(seed), 6)
    return {
        "coords": draw_coords(jax.random.fold_in(seeds[5], 71), 0),
        "final_coords": draw_final_coords(jax.random.fold_in(seeds[5], 71), 0),
        "growth": jnp.clip(jnp.exp(math.log(2.5) - 1.8325814 * jax.random.uniform(seeds[2], (PAIRS, CELLS), jnp.float32) ** block_levels(seeds[2], (PAIRS, CELLS), ((0, 4), (1, 8)), -0.2, 0.2)), 0.4, 2.5),
        "counts": draw_counts(jax.random.fold_in(seeds[5], 71), 0),
        "labels": draw_labels(jax.random.fold_in(seeds[5], 71), 0),
    }


cost_scale = 1.0
source_power = 0.5
target_power = 50.0 / 51.0


def kernel_block(source_block, targets, target_norms):
    cross = lax.dot_general(source_block, targets, (((0,), (0,)), ((), ())), precision=lax.Precision.HIGHEST, preferred_element_type=jnp.float32)
    source_norms = jnp.sum(source_block * source_block, axis=0)
    return jnp.exp(-(source_norms[:, None] + target_norms[None, :] - 2.0 * cross) / cost_scale)


def split_rows(sources, width):
    number = sources.shape[1] // width
    return jnp.transpose(sources.reshape(sources.shape[0], number, width), (1, 0, 2))


def forward(blocks, targets, target_norms, weights):
    def block_out(source_block):
        kernel = kernel_block(source_block, targets, target_norms)
        return lax.dot_general(weights, kernel, (((1,), (1,)), ((), ())), precision=lax.Precision.HIGHEST, preferred_element_type=jnp.float32)

    outputs = lax.map(block_out, blocks)
    return jnp.transpose(outputs, (1, 0, 2)).reshape(weights.shape[0], -1)


def backward(blocks, targets, target_norms, scales):
    scale_blocks = scales.reshape(blocks.shape[0], blocks.shape[2])

    def block_in(pieces):
        kernel = kernel_block(pieces[0], targets, target_norms)
        return jnp.dot(pieces[1], kernel, precision=lax.Precision.HIGHEST, preferred_element_type=jnp.float32)

    return jnp.sum(lax.map(block_in, (blocks, scale_blocks)), axis=0)


def reference(coords, final_coords, growth, counts, labels):
    pairs = coords.shape[0]
    cells = coords.shape[2]
    width = min(512, cells)
    index = lax.iota(jnp.int32, cells)
    saved = []
    masses = []
    for pair in range(pairs):
        sources = coords[pair]
        targets = coords[pair + 1] if pair + 1 < pairs else final_coords
        source_valid = index < counts[pair]
        target_valid = index < counts[pair + 1]
        source_total = counts[pair].astype(jnp.float32)
        target_total = counts[pair + 1].astype(jnp.float32)
        blocks = split_rows(sources, width)
        target_norms = jnp.sum(targets * targets, axis=0)
        start_rows = forward(blocks, targets, target_norms, target_valid.astype(jnp.float32)[None, :])[0]
        source_mass = jnp.where(source_valid, growth[pair] / source_total, 0.0)
        scale_u = jnp.where(source_valid, jnp.power(source_mass / start_rows, source_power), 0.0)
        column_totals = backward(blocks, targets, target_norms, scale_u)
        target_mass = target_valid.astype(jnp.float32) / target_total
        scale_v = jnp.where(target_valid, jnp.power(target_mass / column_totals, target_power), 0.0)
        row_totals = forward(blocks, targets, target_norms, scale_v[None, :])[0]
        masses.append(jnp.where(source_valid, source_total * scale_u * row_totals, 0.0))
        saved.append((blocks, targets, target_norms, scale_v, row_totals, source_valid))
    classes = lax.iota(jnp.int32, CLASSES)
    final_valid = index < counts[pairs]
    carried = jnp.where((labels[None, :] == classes[:, None]) & final_valid[None, :], 1.0, 0.0).astype(jnp.float32)
    results = [None] * pairs
    for pair in range(pairs - 1, -1, -1):
        blocks, targets, target_norms, scale_v, row_totals, source_valid = saved[pair]
        terms = forward(blocks, targets, target_norms, carried * scale_v[None, :])
        carried = jnp.where(source_valid[None, :], terms / jnp.where(source_valid, row_totals, 1.0)[None, :], 0.0)
        results[pair] = carried
    return jnp.stack(results), jnp.stack(masses)
```

```python
import functools
import jax
import jax.numpy as jnp
from jax import lax
from jax.experimental import pallas as pl
from jax.experimental.pallas import tpu as pltpu
from jax.sharding import PartitionSpec as P

CLASSES = 16
FUSED_BYTES = 16 * 1024 * 1024


cost_scale = 1.0
source_power = 0.5
target_power = 50.0 / 51.0


def shifted_2(block, axis, distance):
    devices = range(lax.axis_size(axis))
    route = [(i - distance, i) for i in devices if i - distance in devices]
    return lax.ppermute(block, axis, route)


def kernel_tile(sources, targets):
    cross = lax.dot_general(
        sources,
        targets,
        (((0,), (0,)), ((), ())),
        precision=lax.Precision.HIGHEST,
        preferred_element_type=jnp.float32,
    )
    source_norms = jnp.sum(sources * sources, axis=0)
    target_norms = jnp.sum(targets * targets, axis=0)
    return jnp.exp(-(source_norms[:, None] + target_norms[None, :] - 2.0 * cross) / cost_scale)


def forward(kernel, weights):
    return lax.dot_general(
        weights,
        kernel,
        (((1,), (1,)), ((), ())),
        precision=lax.Precision.HIGHEST,
        preferred_element_type=jnp.float32,
    )


def backward(kernel, scales):
    return jnp.dot(
        scales, kernel, precision=lax.Precision.HIGHEST, preferred_element_type=jnp.float32
    )


def per_device(coords, final_coords, growth, counts, labels):
    tile = coords.shape[2]
    n_pair = lax.axis_size("pair")
    n_row = lax.axis_size("row")
    n_col = lax.axis_size("col")
    pair_at = lax.axis_index("pair")
    row_at = lax.axis_index("row")
    col_at = lax.axis_index("col")
    source_count = n_col * tile
    target_count = n_row * tile
    own_coords = coords[0]
    sources, source_growth = (
        lax.all_gather(own_coords, "col", axis=1, tiled=True),
        lax.all_gather(growth[0], "col", axis=0, tiled=True),
    )
    shifted = shifted_2(own_coords, "pair", -1)
    is_last = pair_at == n_pair - 1
    own_targets = jnp.where(is_last, final_coords, shifted)
    label_values = labels.astype(jnp.float32)
    position = lax.iota(jnp.int32, target_count)
    targets, target_labels = (
        lax.all_gather(own_targets, "row", axis=1, tiled=True),
        lax.all_gather(label_values, "row", axis=0, tiled=True),
    )
    target_index = position // tile * (n_col * tile) + col_at * tile + position % tile

    def hand_over(fates_now):
        incoming = shifted_2(fates_now, "pair", -1)
        return lax.all_gather(incoming, "row", axis=1, tiled=True)

    source_number = counts[pair_at]
    target_number = counts[pair_at + 1]
    source_total = source_number.astype(jnp.float32)
    target_total = target_number.astype(jnp.float32)
    source_index = row_at * source_count + lax.iota(jnp.int32, source_count)
    source_valid = source_index < source_number
    target_valid = target_index < target_number
    kernel = kernel_tile(sources, targets)
    start_terms = forward(kernel, target_valid.astype(jnp.float32)[None, :])[0]
    start_rows = lax.psum(start_terms, "col")
    source_mass = jnp.where(source_valid, source_growth / source_total, 0.0)
    scale_u = jnp.where(source_valid, jnp.power(source_mass / start_rows, source_power), 0.0)
    column_terms = backward(kernel, scale_u)
    column_totals = lax.psum(column_terms, "row")
    target_mass = target_valid.astype(jnp.float32) / target_total
    scale_v = jnp.where(target_valid, jnp.power(target_mass / column_totals, target_power), 0.0)
    own_offset = col_at * tile
    own_valid = lax.dynamic_slice_in_dim(source_valid, own_offset, tile, 0)
    own_scale = lax.dynamic_slice_in_dim(scale_u, own_offset, tile, 0)
    class_values = lax.iota(jnp.int32, CLASSES).astype(jnp.float32)
    label_table = jnp.where(
        (target_labels[None, :] == class_values[:, None]) & target_valid[None, :], 1.0, 0.0
    ).astype(jnp.float32)
    empty = jnp.zeros((CLASSES, tile), jnp.float32)
    final_terms = forward(kernel, scale_v[None, :])[0]
    final_rows = lax.psum(final_terms, "col")
    own_rows = lax.dynamic_slice_in_dim(final_rows, own_offset, tile, 0)
    safe_rows = jnp.where(own_valid, own_rows, 1.0)

    def advance(turn, fates_now):
        carried = jnp.where(is_last, label_table, hand_over(fates_now))
        terms = forward(kernel, carried * scale_v[None, :])
        sums = lax.psum_scatter(terms, "col", scatter_dimension=1, tiled=True)
        return jnp.where(own_valid[None, :], sums / safe_rows[None, :], 0.0)

    fates = lax.fori_loop(0, n_pair, advance, empty)
    mass = jnp.where(own_valid, source_total * own_scale * own_rows, 0.0)
    return (fates[None], mass[None])


LANES = 128
HALF = 16
BIG = 1e30
MESH = pl.DeviceIdType.MESH


def split3(a):
    first = a.astype(jnp.bfloat16)
    rest = a - first.astype(jnp.float32)
    second = rest.astype(jnp.bfloat16)
    third = (rest - second.astype(jnp.float32)).astype(jnp.bfloat16)
    return first, second, third


def split2(a):
    first = a.astype(jnp.bfloat16)
    return first, (a - first.astype(jnp.float32)).astype(jnp.bfloat16)


def dot(a, b, dims):
    return lax.dot_general(a, b, (dims, ((), ())), preferred_element_type=jnp.float32)


def packed(block, extra):
    low = block[:HALF]
    rest = block.shape[0] - HALF
    fill = jnp.zeros((HALF - rest - 1, block.shape[1]), jnp.float32)
    high = jnp.concatenate([block[HALF:], extra, fill], axis=0)
    return jnp.concatenate([low, high], axis=1)


def unpacked(ref):
    lows, highs = [], []
    lane = lax.broadcasted_iota(jnp.int32, (HALF, LANES), 1)
    for j in range(ref.shape[0] // 2):
        a, b = ref[2 * j], ref[2 * j + 1]
        swap_a, swap_b = pltpu.roll(a, LANES // 2, 1), pltpu.roll(b, LANES // 2, 1)
        lows.append(jnp.where(lane < LANES // 2, a, swap_b))
        highs.append(jnp.where(lane < LANES // 2, swap_a, b))
    low, high = jnp.concatenate(lows, axis=1), jnp.concatenate(highs, axis=1)
    return jnp.concatenate([low, high], axis=0)


def own_part(ref, value, mine, tile):
    for j in range(ref.shape[0]):
        ref[j] = value[:, j * LANES : (j + 1) * LANES]
    chunk = ref[mine // 2]
    return pltpu.roll(chunk, (mine % 2) * tile, 1)[:, :tile]


def fused(
    sizes,
    counts_ref,
    coords_ref,
    final_ref,
    growth_ref,
    labels_ref,
    fates_ref,
    mass_ref,
    xg,
    yg,
    k1,
    k2,
    fin,
    fout,
    pick_f,
    pick_m,
    x_send,
    x_recv,
    y_send,
    y_recv,
    f_send,
    f_recv,
):
    n_pair, n_row, n_col, tile = sizes
    n_block = n_row * n_col
    cells = n_block * tile
    pca = coords_ref.shape[1]
    last = n_pair - 1
    pair_at = lax.axis_index("pair")
    row_at = lax.axis_index("row")
    col_at = lax.axis_index("col")
    mine = row_at * n_col + col_at
    is_last = pair_at == last
    not_last = pair_at < last
    not_first = pair_at > 0

    def peer(step):
        other = lax.rem(mine + step, n_block)
        return other, other // n_col, lax.rem(other, n_col)

    barrier = pltpu.get_barrier_semaphore()
    for step in range(1, n_block):
        _, r, c = peer(step)
        pl.semaphore_signal(barrier, inc=1, device_id=(pair_at, r, c), device_id_type=MESH)

    @pl.when(not_last)
    def _():
        for step in range(n_block):
            _, r, c = peer(step)
            pl.semaphore_signal(
                barrier, inc=1, device_id=(pair_at + 1, r, c), device_id_type=MESH
            )

    xg[mine] = packed(coords_ref[0], growth_ref[...])

    @pl.when(is_last)
    def _():
        yg[mine] = packed(final_ref[...], labels_ref[...].astype(jnp.float32))

    @pl.when(not_first)
    def _():
        pl.semaphore_wait(barrier, 2 * n_block - 1)

    @pl.when(pair_at == 0)
    def _():
        pl.semaphore_wait(barrier, n_block - 1)

    def x_copy(step):
        other, r, c = peer(step)
        return pltpu.make_async_remote_copy(
            src_ref=xg.at[mine],
            dst_ref=xg.at[mine],
            send_sem=x_send.at[step],
            recv_sem=x_recv.at[mine],
            device_id=(pair_at, r, c),
            device_id_type=MESH,
        )

    def y_copy(step, source, pair):
        other, r, c = peer(step)
        return pltpu.make_async_remote_copy(
            src_ref=source.at[mine],
            dst_ref=yg.at[mine],
            send_sem=y_send.at[step],
            recv_sem=y_recv.at[mine],
            device_id=(pair, r, c),
            device_id_type=MESH,
        )

    def arrival(buffer, sems, other):
        return pltpu.make_async_remote_copy(
            src_ref=buffer.at[other],
            dst_ref=buffer.at[other],
            send_sem=x_send.at[0],
            recv_sem=sems.at[other],
            device_id=(pair_at, row_at, col_at),
            device_id_type=MESH,
        )

    for step in range(1, n_block):
        x_copy(step).start()

    @pl.when(not_first)
    def _():
        for step in range(n_block):
            y_copy(step, xg, pair_at - 1).start()

    z_send = f_send

    @pl.when(is_last)
    def _():
        for step in range(1, n_block):
            other, r, c = peer(step)
            pltpu.make_async_remote_copy(
                src_ref=yg.at[mine],
                dst_ref=yg.at[mine],
                send_sem=z_send.at[step],
                recv_sem=y_recv.at[mine],
                device_id=(pair_at, r, c),
                device_id_type=MESH,
            ).start()

    for step in range(1, n_block):
        other, _, _ = peer(step)
        arrival(xg, x_recv, other).wait_recv()
    for step in range(1, n_block):
        other, _, _ = peer(step)
        arrival(yg, y_recv, other).wait_recv()

    @pl.when(not_last)
    def _():
        arrival(yg, y_recv, mine).wait_recv()

    source_number = counts_ref[pair_at]
    target_number = counts_ref[pair_at + 1]
    source_total = source_number.astype(jnp.float32)
    target_total = target_number.astype(jnp.float32)
    index = lax.broadcasted_iota(jnp.int32, (1, cells), 1)
    source_valid = index < source_number
    target_valid = index < target_number

    x = unpacked(xg)
    y = unpacked(yg)
    growth = x[pca : pca + 1]
    labels = y[pca : pca + 1]
    feature = lax.broadcasted_iota(jnp.int32, x.shape, 0)
    x = jnp.where(feature < pca, x, 0.0)
    y = jnp.where(feature < pca, y, 0.0)
    x_norm = jnp.sum(x * x, axis=0, keepdims=True)
    y_norm = jnp.where(target_valid, jnp.sum(y * y, axis=0, keepdims=True), BIG)
    a = jnp.where(feature < pca, x + x, jnp.where(feature == pca, -x_norm, 1.0))
    b = jnp.where(feature < pca, y, jnp.where(feature == pca, 1.0, -y_norm))
    a1, a2, a3 = split3(a)
    b1, b2, b3 = split3(b)
    left = jnp.concatenate([b1, b1, b2, b2, b1, b3], axis=0)
    right = jnp.concatenate([a1, a2, a1, a2, a3, a1], axis=0)
    totals = jnp.zeros((1, cells), jnp.float32)
    for j in range(cells // LANES):
        rows = slice(j * LANES, (j + 1) * LANES)
        values = jnp.exp(dot(left[:, rows], right, ((0,), (0,))))
        totals = totals + jnp.sum(values, axis=0, keepdims=True)
        high, low = split2(values)
        k1[rows, :] = high
        k2[rows, :] = low
    scale_u = jnp.where(source_valid, jnp.sqrt(growth / source_total / totals), 0.0)
    u1, u2 = split2(jnp.broadcast_to(scale_u, (HALF, cells)))
    u12 = jnp.concatenate([u1, u2], axis=0)
    column = dot(u12, k1[...], ((1,), (1,)))
    column_low = dot(u1, k2[...], ((1,), (1,)))
    column = column[:1] + column[HALF : HALF + 1] + column_low[:1]
    ratio = 1.0 / target_total / jnp.where(target_valid, column, 1.0)
    scale_v = jnp.where(target_valid, jnp.exp(target_power * jnp.log(ratio)), 0.0)

    def transported(weights):
        w1, w2 = split2(weights)
        both = dot(jnp.concatenate([w1, w2], axis=0), k1[...], ((1,), (0,)))
        return both[:CLASSES] + both[CLASSES:] + dot(w1, k2[...], ((1,), (0,)))

    row_totals = transported(jnp.broadcast_to(scale_v, (CLASSES, cells)))[:1]
    mass = jnp.where(source_valid, source_total * scale_u * row_totals, 0.0)
    mass_ref[...] = own_part(pick_m, jnp.broadcast_to(mass, (8, cells)), mine, tile)[:1]
    share = jnp.where(source_valid, 1.0 / row_totals, 0.0)

    f_copy = pltpu.make_async_remote_copy(
        src_ref=fout,
        dst_ref=fin,
        send_sem=f_send.at[0],
        recv_sem=f_recv,
        device_id=(jnp.maximum(pair_at - 1, 0), row_at, col_at),
        device_id_type=MESH,
    )

    @pl.when(is_last)
    def _():
        class_values = lax.broadcasted_iota(jnp.int32, (CLASSES, cells), 0).astype(jnp.float32)
        fin[...] = jnp.where((labels == class_values) & target_valid, 1.0, 0.0)

    @pl.when(not_last)
    def _():
        f_copy.wait_recv()

    fates = transported(fin[...] * scale_v) * share
    fout[...] = fates

    @pl.when(not_first)
    def _():
        f_copy.start()

    fates_ref[0] = own_part(pick_f, fates, mine, tile)

    for step in range(1, n_block):
        x_copy(step).wait_send()

    @pl.when(not_first)
    def _():
        for step in range(n_block):
            y_copy(step, xg, pair_at - 1).wait_send()
        f_copy.wait_send()

    @pl.when(is_last)
    def _():
        for step in range(1, n_block):
            pltpu.make_async_remote_copy(
                src_ref=yg.at[mine],
                dst_ref=yg.at[mine],
                send_sem=z_send.at[step],
                recv_sem=y_recv.at[mine],
                device_id=(pair_at, row_at, col_at),
                device_id_type=MESH,
            ).wait_send()


def per_device_fused(coords, final_coords, growth, counts, labels):
    tile = coords.shape[2]
    n_pair = lax.axis_size("pair")
    n_row = lax.axis_size("row")
    n_col = lax.axis_size("col")
    n_block = n_row * n_col
    cells = n_block * tile
    vmem = pl.BlockSpec(memory_space=pltpu.VMEM)
    dma = pltpu.SemaphoreType.DMA
    return pl.pallas_call(
        functools.partial(fused, (n_pair, n_row, n_col, tile)),
        out_shape=(
            jax.ShapeDtypeStruct((1, CLASSES, tile), jnp.float32),
            jax.ShapeDtypeStruct((1, tile), jnp.float32),
        ),
        in_specs=[pl.BlockSpec(memory_space=pltpu.SMEM), vmem, vmem, vmem, vmem],
        out_specs=(vmem, vmem),
        scratch_shapes=[
            pltpu.VMEM((n_block, HALF, LANES), jnp.float32),
            pltpu.VMEM((n_block, HALF, LANES), jnp.float32),
            pltpu.VMEM((cells, cells), jnp.bfloat16),
            pltpu.VMEM((cells, cells), jnp.bfloat16),
            pltpu.VMEM((CLASSES, cells), jnp.float32),
            pltpu.VMEM((CLASSES, cells), jnp.float32),
            pltpu.VMEM((cells // LANES, CLASSES, LANES), jnp.float32),
            pltpu.VMEM((cells // LANES, 8, LANES), jnp.float32),
            dma((n_block,)),
            dma((n_block,)),
            dma((n_block,)),
            dma((n_block,)),
            dma((n_block,)),
            dma,
        ],
        compiler_params=pltpu.CompilerParams(collective_id=0, has_side_effects=True),
    )(counts, coords, final_coords, growth, labels[None, :])


def solution(mesh):
    placed = (
        P("pair", None, ("row", "col")),
        P(None, ("row", "col")),
        P("pair", ("row", "col")),
        P(),
        P(("row", "col")),
    )
    out = (P("pair", None, ("row", "col")), P("pair", ("row", "col")))

    def whole(coords, final_coords, growth, counts, labels):
        cells = coords.shape[2]
        blocks = mesh.shape["row"] * mesh.shape["col"]
        fits = (
            2 * cells == LANES * blocks
            and blocks % 2 == 0
            and coords.shape[0] == mesh.shape["pair"]
            and HALF < coords.shape[1] < 2 * HALF - 1
            and 4 * cells * cells <= FUSED_BYTES
        )
        body = per_device_fused if fits else per_device
        return jax.shard_map(
            body, mesh=mesh, in_specs=placed, out_specs=out, check_vma=False
        )(coords, final_coords, growth, counts, labels)

    return whole
```

```python
import functools
import jax
import jax.numpy as jnp
from jax import lax
from jax.experimental import pallas as pl
from jax.experimental.pallas import tpu as pltpu
from jax.sharding import PartitionSpec as P

CLASSES = 16
FUSED_BYTES = 16 * 1024 * 1024


cost_scale = 1.0
source_power = 0.5
target_power = 50.0 / 51.0


def shifted_2(block, axis, distance):
    devices = range(lax.axis_size(axis))
    route = [(i - distance, i) for i in devices if i - distance in devices]
    return lax.ppermute(block, axis, route)


def kernel_tile(sources, targets):
    cross = lax.dot_general(
        sources,
        targets,
        (((0,), (0,)), ((), ())),
        precision=lax.Precision.HIGHEST,
        preferred_element_type=jnp.float32,
    )
    source_norms = jnp.sum(sources * sources, axis=0)
    target_norms = jnp.sum(targets * targets, axis=0)
    return jnp.exp(-(source_norms[:, None] + target_norms[None, :] - 2.0 * cross) / cost_scale)


def forward(kernel, weights):
    return lax.dot_general(
        weights,
        kernel,
        (((1,), (1,)), ((), ())),
        precision=lax.Precision.HIGHEST,
        preferred_element_type=jnp.float32,
    )


def backward(kernel, scales):
    return jnp.dot(
        scales, kernel, precision=lax.Precision.HIGHEST, preferred_element_type=jnp.float32
    )


def per_device(coords, final_coords, growth, counts, labels):
    tile = coords.shape[2]
    n_pair = lax.axis_size("pair")
    n_row = lax.axis_size("row")
    n_col = lax.axis_size("col")
    pair_at = lax.axis_index("pair")
    row_at = lax.axis_index("row")
    col_at = lax.axis_index("col")
    source_count = n_col * tile
    target_count = n_row * tile
    own_coords = coords[0]
    sources, source_growth = (
        lax.all_gather(own_coords, "col", axis=1, tiled=True),
        lax.all_gather(growth[0], "col", axis=0, tiled=True),
    )
    shifted = shifted_2(own_coords, "pair", -1)
    is_last = pair_at == n_pair - 1
    own_targets = jnp.where(is_last, final_coords, shifted)
    label_values = labels.astype(jnp.float32)
    position = lax.iota(jnp.int32, target_count)
    targets, target_labels = (
        lax.all_gather(own_targets, "row", axis=1, tiled=True),
        lax.all_gather(label_values, "row", axis=0, tiled=True),
    )
    target_index = position // tile * (n_col * tile) + col_at * tile + position % tile

    def hand_over(fates_now):
        incoming = shifted_2(fates_now, "pair", -1)
        return lax.all_gather(incoming, "row", axis=1, tiled=True)

    source_number = counts[pair_at]
    target_number = counts[pair_at + 1]
    source_total = source_number.astype(jnp.float32)
    target_total = target_number.astype(jnp.float32)
    source_index = row_at * source_count + lax.iota(jnp.int32, source_count)
    source_valid = source_index < source_number
    target_valid = target_index < target_number
    kernel = kernel_tile(sources, targets)
    start_terms = forward(kernel, target_valid.astype(jnp.float32)[None, :])[0]
    start_rows = lax.psum(start_terms, "col")
    source_mass = jnp.where(source_valid, source_growth / source_total, 0.0)
    scale_u = jnp.where(source_valid, jnp.power(source_mass / start_rows, source_power), 0.0)
    column_terms = backward(kernel, scale_u)
    column_totals = lax.psum(column_terms, "row")
    target_mass = target_valid.astype(jnp.float32) / target_total
    scale_v = jnp.where(target_valid, jnp.power(target_mass / column_totals, target_power), 0.0)
    own_offset = col_at * tile
    own_valid = lax.dynamic_slice_in_dim(source_valid, own_offset, tile, 0)
    own_scale = lax.dynamic_slice_in_dim(scale_u, own_offset, tile, 0)
    class_values = lax.iota(jnp.int32, CLASSES).astype(jnp.float32)
    label_table = jnp.where(
        (target_labels[None, :] == class_values[:, None]) & target_valid[None, :], 1.0, 0.0
    ).astype(jnp.float32)
    empty = jnp.zeros((CLASSES, tile), jnp.float32)
    final_terms = forward(kernel, scale_v[None, :])[0]
    final_rows = lax.psum(final_terms, "col")
    own_rows = lax.dynamic_slice_in_dim(final_rows, own_offset, tile, 0)
    safe_rows = jnp.where(own_valid, own_rows, 1.0)

    def advance(turn, fates_now):
        carried = jnp.where(is_last, label_table, hand_over(fates_now))
        terms = forward(kernel, carried * scale_v[None, :])
        sums = lax.psum_scatter(terms, "col", scatter_dimension=1, tiled=True)
        return jnp.where(own_valid[None, :], sums / safe_rows[None, :], 0.0)

    fates = lax.fori_loop(0, n_pair, advance, empty)
    mass = jnp.where(own_valid, source_total * own_scale * own_rows, 0.0)
    return (fates[None], mass[None])


LANES = 128
HALF = 16
BIG = 1e30
MESH = pl.DeviceIdType.MESH


def split3(a):
    first = a.astype(jnp.bfloat16)
    rest = a - first.astype(jnp.float32)
    second = rest.astype(jnp.bfloat16)
    third = (rest - second.astype(jnp.float32)).astype(jnp.bfloat16)
    return first, second, third


def split2(a):
    first = a.astype(jnp.bfloat16)
    return first, (a - first.astype(jnp.float32)).astype(jnp.bfloat16)


def dot(a, b, dims):
    return lax.dot_general(a, b, (dims, ((), ())), preferred_element_type=jnp.float32)


def packed(block, extra):
    low = block[:HALF]
    rest = block.shape[0] - HALF
    fill = jnp.zeros((HALF - rest - 1, block.shape[1]), jnp.float32)
    high = jnp.concatenate([block[HALF:], extra, fill], axis=0)
    return jnp.concatenate([low, high], axis=1)


def unpacked(ref):
    lows, highs = [], []
    lane = lax.broadcasted_iota(jnp.int32, (HALF, LANES), 1)
    for j in range(ref.shape[0] // 2):
        a, b = ref[2 * j], ref[2 * j + 1]
        swap_a, swap_b = pltpu.roll(a, LANES // 2, 1), pltpu.roll(b, LANES // 2, 1)
        lows.append(jnp.where(lane < LANES // 2, a, swap_b))
        highs.append(jnp.where(lane < LANES // 2, swap_a, b))
    low, high = jnp.concatenate(lows, axis=1), jnp.concatenate(highs, axis=1)
    return jnp.concatenate([low, high], axis=0)


def own_part(ref, value, mine, tile):
    for j in range(ref.shape[0]):
        ref[j] = value[:, j * LANES : (j + 1) * LANES]
    chunk = ref[mine // 2]
    return pltpu.roll(chunk, (mine % 2) * tile, 1)[:, :tile]


def fused(
    sizes,
    counts_ref,
    coords_ref,
    final_ref,
    growth_ref,
    labels_ref,
    fates_ref,
    mass_ref,
    xg,
    yg,
    k1,
    k2,
    fin,
    fout,
    pick_f,
    pick_m,
    x_send,
    x_recv,
    y_send,
    y_recv,
    z_send,
    f_send,
    f_recv,
):
    n_pair, n_row, n_col, tile = sizes
    n_block = n_row * n_col
    cells = n_block * tile
    pca = coords_ref.shape[0]
    last = n_pair - 1
    pair_at = lax.axis_index("pair")
    row_at = lax.axis_index("row")
    col_at = lax.axis_index("col")
    mine = row_at * n_col + col_at
    is_last = pair_at == last
    not_last = pair_at < last
    not_first = pair_at > 0

    def peer(step):
        other = lax.rem(mine + step, n_block)
        return other, other // n_col, lax.rem(other, n_col)

    barrier = pltpu.get_barrier_semaphore()
    for step in range(1, n_block):
        _, r, c = peer(step)
        pl.semaphore_signal(barrier, inc=1, device_id=(pair_at, r, c), device_id_type=MESH)

    @pl.when(not_last)
    def _():
        pl.semaphore_signal(
            barrier, inc=1, device_id=(pair_at + 1, row_at, col_at), device_id_type=MESH
        )

    xg[mine] = packed(coords_ref[:, 0, :], growth_ref[...])

    @pl.when(is_last)
    def _():
        yg[mine] = packed(final_ref[...], labels_ref[...].astype(jnp.float32))

    @pl.when(not_first)
    def _():
        pl.semaphore_wait(barrier, n_block)

    @pl.when(pair_at == 0)
    def _():
        pl.semaphore_wait(barrier, n_block - 1)

    def x_copy(step):
        other, r, c = peer(step)
        return pltpu.make_async_remote_copy(
            src_ref=xg.at[mine],
            dst_ref=xg.at[mine],
            send_sem=x_send.at[step],
            recv_sem=x_recv.at[mine],
            device_id=(pair_at, r, c),
            device_id_type=MESH,
        )

    def final_copy(step):
        other, r, c = peer(step)
        return pltpu.make_async_remote_copy(
            src_ref=yg.at[mine],
            dst_ref=yg.at[mine],
            send_sem=z_send.at[step],
            recv_sem=y_recv.at[mine],
            device_id=(pair_at, r, c),
            device_id_type=MESH,
        )

    def relay(block):
        return pltpu.make_async_remote_copy(
            src_ref=xg.at[block],
            dst_ref=yg.at[block],
            send_sem=y_send.at[block],
            recv_sem=y_recv.at[block],
            device_id=(jnp.maximum(pair_at - 1, 0), row_at, col_at),
            device_id_type=MESH,
        )

    def arrival(buffer, sems, other):
        return pltpu.make_async_remote_copy(
            src_ref=buffer.at[other],
            dst_ref=buffer.at[other],
            send_sem=x_send.at[0],
            recv_sem=sems.at[other],
            device_id=(pair_at, row_at, col_at),
            device_id_type=MESH,
        )

    for step in range(1, n_block):
        x_copy(step).start()

        @pl.when(is_last)
        def _(step=step):
            final_copy(step).start()

    for block in range(n_block):

        @pl.when(mine != block)
        def _(block=block):
            arrival(xg, x_recv, block).wait_recv()

        @pl.when(not_first)
        def _(block=block):
            relay(block).start()

    for block in range(n_block):

        @pl.when(not_last | (mine != block))
        def _(block=block):
            arrival(yg, y_recv, block).wait_recv()

    source_number = counts_ref[pair_at]
    target_number = counts_ref[pair_at + 1]
    source_total = source_number.astype(jnp.float32)
    target_total = target_number.astype(jnp.float32)
    index = lax.broadcasted_iota(jnp.int32, (1, cells), 1)
    source_valid = index < source_number
    target_valid = index < target_number

    x = unpacked(xg)
    y = unpacked(yg)
    growth = x[pca : pca + 1]
    labels = y[pca : pca + 1]
    feature = lax.broadcasted_iota(jnp.int32, x.shape, 0)
    x = jnp.where(feature < pca, x, 0.0)
    y = jnp.where(feature < pca, y, 0.0)
    x_norm = jnp.sum(x * x, axis=0, keepdims=True)
    y_norm = jnp.where(target_valid, jnp.sum(y * y, axis=0, keepdims=True), BIG)
    a = jnp.where(feature < pca, x + x, jnp.where(feature == pca, -x_norm, 1.0))
    b = jnp.where(feature < pca, y, jnp.where(feature == pca, 1.0, -y_norm))
    a1, a2, a3 = split3(a)
    b1, b2, b3 = split3(b)
    left = jnp.concatenate([b1, b1, b2, b2, b1, b3], axis=0)
    right = jnp.concatenate([a1, a2, a1, a2, a3, a1], axis=0)
    totals = jnp.zeros((1, cells), jnp.float32)
    for j in range(cells // LANES):
        rows = slice(j * LANES, (j + 1) * LANES)
        values = jnp.exp(dot(left[:, rows], right, ((0,), (0,))))
        totals = totals + jnp.sum(values, axis=0, keepdims=True)
        high, low = split2(values)
        k1[rows, :] = high
        k2[rows, :] = low
    scale_u = jnp.where(source_valid, jnp.sqrt(growth / source_total / totals), 0.0)
    u1, u2 = split2(jnp.broadcast_to(scale_u, (HALF, cells)))
    u12 = jnp.concatenate([u1, u2], axis=0)
    column = dot(u12, k1[...], ((1,), (1,)))
    column_low = dot(u1, k2[...], ((1,), (1,)))
    column = column[:1] + column[HALF : HALF + 1] + column_low[:1]
    ratio = 1.0 / target_total / jnp.where(target_valid, column, 1.0)
    scale_v = jnp.where(target_valid, jnp.exp(target_power * jnp.log(ratio)), 0.0)

    def transported(weights):
        w1, w2 = split2(weights)
        both = dot(jnp.concatenate([w1, w2], axis=0), k1[...], ((1,), (0,)))
        return both[:CLASSES] + both[CLASSES:] + dot(w1, k2[...], ((1,), (0,)))

    row_totals = transported(jnp.broadcast_to(scale_v, (CLASSES, cells)))[:1]
    mass = jnp.where(source_valid, source_total * scale_u * row_totals, 0.0)
    mass_ref[...] = own_part(pick_m, jnp.broadcast_to(mass, (8, cells)), mine, tile)[:1]
    share = jnp.where(source_valid, 1.0 / row_totals, 0.0)

    f_copy = pltpu.make_async_remote_copy(
        src_ref=fout,
        dst_ref=fin,
        send_sem=f_send,
        recv_sem=f_recv,
        device_id=(jnp.maximum(pair_at - 1, 0), row_at, col_at),
        device_id_type=MESH,
    )

    @pl.when(is_last)
    def _():
        class_values = lax.broadcasted_iota(jnp.int32, (CLASSES, cells), 0).astype(jnp.float32)
        fin[...] = jnp.where((labels == class_values) & target_valid, 1.0, 0.0)

    @pl.when(not_last)
    def _():
        f_copy.wait_recv()

    fates = transported(fin[...] * scale_v) * share
    fout[...] = fates

    @pl.when(not_first)
    def _():
        f_copy.start()

    fates_ref[0] = own_part(pick_f, fates, mine, tile)

    for step in range(1, n_block):
        x_copy(step).wait_send()

    @pl.when(not_first)
    def _():
        for block in range(n_block):
            relay(block).wait_send()
        f_copy.wait_send()

    @pl.when(is_last)
    def _():
        for step in range(1, n_block):
            final_copy(step).wait_send()


def per_device_fused(coords, final_coords, growth, counts, labels):
    tile = coords.shape[2]
    n_pair = lax.axis_size("pair")
    n_row = lax.axis_size("row")
    n_col = lax.axis_size("col")
    n_block = n_row * n_col
    cells = n_block * tile
    vmem = pl.BlockSpec(memory_space=pltpu.VMEM)
    dma = pltpu.SemaphoreType.DMA
    return pl.pallas_call(
        functools.partial(fused, (n_pair, n_row, n_col, tile)),
        out_shape=(
            pltpu.VMEM((1, CLASSES, tile), jnp.float32),
            pltpu.VMEM((1, tile), jnp.float32),
        ),
        in_specs=[pl.BlockSpec(memory_space=pltpu.SMEM), vmem, vmem, vmem, vmem],
        out_specs=(vmem, vmem),
        scratch_shapes=[
            pltpu.VMEM((n_block, HALF, LANES), jnp.float32),
            pltpu.VMEM((n_block, HALF, LANES), jnp.float32),
            pltpu.VMEM((cells, cells), jnp.bfloat16),
            pltpu.VMEM((cells, cells), jnp.bfloat16),
            pltpu.VMEM((CLASSES, cells), jnp.float32),
            pltpu.VMEM((CLASSES, cells), jnp.float32),
            pltpu.VMEM((cells // LANES, CLASSES, LANES), jnp.float32),
            pltpu.VMEM((cells // LANES, 8, LANES), jnp.float32),
            dma((n_block,)),
            dma((n_block,)),
            dma((n_block,)),
            dma((n_block,)),
            dma((n_block,)),
            dma,
            dma,
        ],
        compiler_params=pltpu.CompilerParams(collective_id=0, has_side_effects=True),
    )(counts, jnp.transpose(coords, (1, 0, 2)), final_coords, growth, labels[None, :])


def solution(mesh):
    placed = (
        P("pair", None, ("row", "col")),
        P(None, ("row", "col")),
        P("pair", ("row", "col")),
        P(),
        P(("row", "col")),
    )
    out = (P("pair", None, ("row", "col")), P("pair", ("row", "col")))

    def whole(coords, final_coords, growth, counts, labels):
        cells = coords.shape[2]
        blocks = mesh.shape["row"] * mesh.shape["col"]
        fits = (
            2 * cells == LANES * blocks
            and blocks % 2 == 0
            and coords.shape[0] == mesh.shape["pair"]
            and HALF < coords.shape[1] < 2 * HALF - 1
            and 4 * cells * cells <= FUSED_BYTES
        )
        body = per_device_fused if fits else per_device
        return jax.shard_map(
            body, mesh=mesh, in_specs=placed, out_specs=out, check_vma=False
        )(coords, final_coords, growth, counts, labels)

    return whole
```

```python
import functools
import jax
import jax.numpy as jnp
from jax import lax
from jax.experimental import pallas as pl
from jax.experimental.pallas import tpu as pltpu
from jax.sharding import PartitionSpec as P

CLASSES = 16
FUSED_BYTES = 16 * 1024 * 1024


cost_scale = 1.0
source_power = 0.5
target_power = 50.0 / 51.0


def shifted_2(block, axis, distance):
    devices = range(lax.axis_size(axis))
    route = [(i - distance, i) for i in devices if i - distance in devices]
    return lax.ppermute(block, axis, route)


def kernel_tile(sources, targets):
    cross = lax.dot_general(
        sources,
        targets,
        (((0,), (0,)), ((), ())),
        precision=lax.Precision.HIGHEST,
        preferred_element_type=jnp.float32,
    )
    source_norms = jnp.sum(sources * sources, axis=0)
    target_norms = jnp.sum(targets * targets, axis=0)
    return jnp.exp(-(source_norms[:, None] + target_norms[None, :] - 2.0 * cross) / cost_scale)


def forward(kernel, weights):
    return lax.dot_general(
        weights,
        kernel,
        (((1,), (1,)), ((), ())),
        precision=lax.Precision.HIGHEST,
        preferred_element_type=jnp.float32,
    )


def backward(kernel, scales):
    return jnp.dot(
        scales, kernel, precision=lax.Precision.HIGHEST, preferred_element_type=jnp.float32
    )


def per_device(coords, final_coords, growth, counts, labels):
    tile = coords.shape[2]
    n_pair = lax.axis_size("pair")
    n_row = lax.axis_size("row")
    n_col = lax.axis_size("col")
    pair_at = lax.axis_index("pair")
    row_at = lax.axis_index("row")
    col_at = lax.axis_index("col")
    source_count = n_col * tile
    target_count = n_row * tile
    own_coords = coords[0]
    sources, source_growth = (
        lax.all_gather(own_coords, "col", axis=1, tiled=True),
        lax.all_gather(growth[0], "col", axis=0, tiled=True),
    )
    shifted = shifted_2(own_coords, "pair", -1)
    is_last = pair_at == n_pair - 1
    own_targets = jnp.where(is_last, final_coords, shifted)
    label_values = labels.astype(jnp.float32)
    position = lax.iota(jnp.int32, target_count)
    targets, target_labels = (
        lax.all_gather(own_targets, "row", axis=1, tiled=True),
        lax.all_gather(label_values, "row", axis=0, tiled=True),
    )
    target_index = position // tile * (n_col * tile) + col_at * tile + position % tile

    def hand_over(fates_now):
        incoming = shifted_2(fates_now, "pair", -1)
        return lax.all_gather(incoming, "row", axis=1, tiled=True)

    source_number = counts[pair_at]
    target_number = counts[pair_at + 1]
    source_total = source_number.astype(jnp.float32)
    target_total = target_number.astype(jnp.float32)
    source_index = row_at * source_count + lax.iota(jnp.int32, source_count)
    source_valid = source_index < source_number
    target_valid = target_index < target_number
    kernel = kernel_tile(sources, targets)
    start_terms = forward(kernel, target_valid.astype(jnp.float32)[None, :])[0]
    start_rows = lax.psum(start_terms, "col")
    source_mass = jnp.where(source_valid, source_growth / source_total, 0.0)
    scale_u = jnp.where(source_valid, jnp.power(source_mass / start_rows, source_power), 0.0)
    column_terms = backward(kernel, scale_u)
    column_totals = lax.psum(column_terms, "row")
    target_mass = target_valid.astype(jnp.float32) / target_total
    scale_v = jnp.where(target_valid, jnp.power(target_mass / column_totals, target_power), 0.0)
    own_offset = col_at * tile
    own_valid = lax.dynamic_slice_in_dim(source_valid, own_offset, tile, 0)
    own_scale = lax.dynamic_slice_in_dim(scale_u, own_offset, tile, 0)
    class_values = lax.iota(jnp.int32, CLASSES).astype(jnp.float32)
    label_table = jnp.where(
        (target_labels[None, :] == class_values[:, None]) & target_valid[None, :], 1.0, 0.0
    ).astype(jnp.float32)
    empty = jnp.zeros((CLASSES, tile), jnp.float32)
    final_terms = forward(kernel, scale_v[None, :])[0]
    final_rows = lax.psum(final_terms, "col")
    own_rows = lax.dynamic_slice_in_dim(final_rows, own_offset, tile, 0)
    safe_rows = jnp.where(own_valid, own_rows, 1.0)

    def advance(turn, fates_now):
        carried = jnp.where(is_last, label_table, hand_over(fates_now))
        terms = forward(kernel, carried * scale_v[None, :])
        sums = lax.psum_scatter(terms, "col", scatter_dimension=1, tiled=True)
        return jnp.where(own_valid[None, :], sums / safe_rows[None, :], 0.0)

    fates = lax.fori_loop(0, n_pair, advance, empty)
    mass = jnp.where(own_valid, source_total * own_scale * own_rows, 0.0)
    return (fates[None], mass[None])


LANES = 128
HALF = 16
BIG = 1e30
MESH = pl.DeviceIdType.MESH


def split3(a):
    first = a.astype(jnp.bfloat16)
    rest = a - first.astype(jnp.float32)
    second = rest.astype(jnp.bfloat16)
    third = (rest - second.astype(jnp.float32)).astype(jnp.bfloat16)
    return first, second, third


def split2(a):
    first = a.astype(jnp.bfloat16)
    return first, (a - first.astype(jnp.float32)).astype(jnp.bfloat16)


def dot(a, b, dims):
    return lax.dot_general(a, b, (dims, ((), ())), preferred_element_type=jnp.float32)


def packed(block, extra):
    low = block[:HALF]
    rest = block.shape[0] - HALF
    fill = jnp.zeros((HALF - rest - 1, block.shape[1]), jnp.float32)
    high = jnp.concatenate([block[HALF:], extra, fill], axis=0)
    return jnp.concatenate([low, high], axis=1)


def unpacked(ref):
    lows, highs = [], []
    lane = lax.broadcasted_iota(jnp.int32, (HALF, LANES), 1)
    for j in range(ref.shape[0] // 2):
        a, b = ref[2 * j], ref[2 * j + 1]
        swap_a, swap_b = pltpu.roll(a, LANES // 2, 1), pltpu.roll(b, LANES // 2, 1)
        lows.append(jnp.where(lane < LANES // 2, a, swap_b))
        highs.append(jnp.where(lane < LANES // 2, swap_a, b))
    low, high = jnp.concatenate(lows, axis=1), jnp.concatenate(highs, axis=1)
    return jnp.concatenate([low, high], axis=0)


def own_part(ref, value, mine, tile):
    for j in range(ref.shape[0]):
        ref[j] = value[:, j * LANES : (j + 1) * LANES]
    chunk = ref[mine // 2]
    return pltpu.roll(chunk, (mine % 2) * tile, 1)[:, :tile]


def fused(
    sizes,
    counts_ref,
    coords_in,
    final_in,
    growth_in,
    labels_in,
    fates_ref,
    mass_ref,
    coords_ref,
    final_ref,
    growth_ref,
    labels_ref,
    in_sems,
    xg,
    yg,
    k1,
    k2,
    fin,
    fout,
    pick_f,
    pick_m,
    x_send,
    x_recv,
    y_send,
    y_recv,
    z_send,
    f_send,
    f_recv,
):
    n_pair, n_row, n_col, tile = sizes
    n_block = n_row * n_col
    cells = n_block * tile
    pca = coords_ref.shape[0]
    last = n_pair - 1
    pair_at = lax.axis_index("pair")
    row_at = lax.axis_index("row")
    col_at = lax.axis_index("col")
    mine = row_at * n_col + col_at
    is_last = pair_at == last
    not_last = pair_at < last
    not_first = pair_at > 0

    def others(act):
        for block in range(n_block):
            pl.when(mine != block)(functools.partial(act, block))

    barrier = pltpu.get_barrier_semaphore()

    @others
    def _(block):
        r, c = divmod(block, n_col)
        pl.semaphore_signal(barrier, inc=1, device_id=(pair_at, r, c), device_id_type=MESH)

    @pl.when(not_last)
    def _():
        pl.semaphore_signal(
            barrier, inc=1, device_id=(pair_at + 1, row_at, col_at), device_id_type=MESH
        )

    source_loads = (
        pltpu.make_async_copy(coords_in, coords_ref, in_sems.at[0]),
        pltpu.make_async_copy(growth_in, growth_ref, in_sems.at[1]),
    )
    target_loads = (
        pltpu.make_async_copy(final_in, final_ref, in_sems.at[2]),
        pltpu.make_async_copy(labels_in, labels_ref, in_sems.at[3]),
    )
    for load in source_loads + target_loads:
        load.start()
    for load in source_loads + target_loads:
        load.wait()
    xg[mine] = packed(coords_ref[:, 0, :], growth_ref[...])

    @pl.when(is_last)
    def _():
        yg[mine] = packed(final_ref[...], labels_ref[...].astype(jnp.float32))

    @pl.when(not_first)
    def _():
        pl.semaphore_wait(barrier, n_block)

    @pl.when(pair_at == 0)
    def _():
        pl.semaphore_wait(barrier, n_block - 1)

    def x_copy(block):
        r, c = divmod(block, n_col)
        return pltpu.make_async_remote_copy(
            src_ref=xg.at[mine],
            dst_ref=xg.at[mine],
            send_sem=x_send.at[block],
            recv_sem=x_recv.at[mine],
            device_id=(pair_at, r, c),
            device_id_type=MESH,
        )

    def final_copy(block):
        r, c = divmod(block, n_col)
        return pltpu.make_async_remote_copy(
            src_ref=yg.at[mine],
            dst_ref=yg.at[mine],
            send_sem=z_send.at[block],
            recv_sem=y_recv.at[mine],
            device_id=(pair_at, r, c),
            device_id_type=MESH,
        )

    def relay(block):
        return pltpu.make_async_remote_copy(
            src_ref=xg.at[block],
            dst_ref=yg.at[block],
            send_sem=y_send.at[block],
            recv_sem=y_recv.at[block],
            device_id=(jnp.maximum(pair_at - 1, 0), row_at, col_at),
            device_id_type=MESH,
        )

    def arrival(buffer, sems, other):
        return pltpu.make_async_remote_copy(
            src_ref=buffer.at[other],
            dst_ref=buffer.at[other],
            send_sem=x_send.at[0],
            recv_sem=sems.at[other],
            device_id=(pair_at, row_at, col_at),
            device_id_type=MESH,
        )

    @others
    def _(block):
        x_copy(block).start()

        @pl.when(is_last)
        def _():
            final_copy(block).start()

    for block in range(n_block):

        @pl.when(mine != block)
        def _(block=block):
            arrival(xg, x_recv, block).wait_recv()

        @pl.when(not_first)
        def _(block=block):
            relay(block).start()

    for block in range(n_block):

        @pl.when(not_last | (mine != block))
        def _(block=block):
            arrival(yg, y_recv, block).wait_recv()

    source_number = counts_ref[pair_at]
    target_number = counts_ref[pair_at + 1]
    source_total = source_number.astype(jnp.float32)
    target_total = target_number.astype(jnp.float32)
    index = lax.broadcasted_iota(jnp.int32, (1, cells), 1)
    source_valid = index < source_number
    target_valid = index < target_number

    x = unpacked(xg)
    y = unpacked(yg)
    growth = x[pca : pca + 1]
    labels = y[pca : pca + 1]
    feature = lax.broadcasted_iota(jnp.int32, x.shape, 0)
    x = jnp.where(feature < pca, x, 0.0)
    y = jnp.where(feature < pca, y, 0.0)
    x_norm = jnp.sum(x * x, axis=0, keepdims=True)
    y_norm = jnp.where(target_valid, jnp.sum(y * y, axis=0, keepdims=True), BIG)
    a = jnp.where(feature < pca, x + x, jnp.where(feature == pca, -x_norm, 1.0))
    b = jnp.where(feature < pca, y, jnp.where(feature == pca, 1.0, -y_norm))
    a1, a2, a3 = split3(a)
    b1, b2, b3 = split3(b)
    left = jnp.concatenate([b1, b1, b2, b2, b1, b3], axis=0)
    right = jnp.concatenate([a1, a2, a1, a2, a3, a1], axis=0)
    totals = jnp.zeros((1, cells), jnp.float32)
    for j in range(cells // LANES):
        rows = slice(j * LANES, (j + 1) * LANES)
        values = jnp.exp(dot(left[:, rows], right, ((0,), (0,))))
        totals = totals + jnp.sum(values, axis=0, keepdims=True)
        high, low = split2(values)
        k1[rows, :] = high
        k2[rows, :] = low
    scale_u = jnp.where(source_valid, jnp.sqrt(growth / source_total / totals), 0.0)
    u1, u2 = split2(jnp.broadcast_to(scale_u, (HALF, cells)))
    u12 = jnp.concatenate([u1, u2], axis=0)
    column = dot(u12, k1[...], ((1,), (1,)))
    column_low = dot(u1, k2[...], ((1,), (1,)))
    column = column[:1] + column[HALF : HALF + 1] + column_low[:1]
    ratio = 1.0 / target_total / jnp.where(target_valid, column, 1.0)
    scale_v = jnp.where(target_valid, jnp.exp(target_power * jnp.log(ratio)), 0.0)

    def transported(weights):
        w1, w2 = split2(weights)
        both = dot(jnp.concatenate([w1, w2], axis=0), k1[...], ((1,), (0,)))
        return both[:CLASSES] + both[CLASSES:] + dot(w1, k2[...], ((1,), (0,)))

    row_totals = transported(jnp.broadcast_to(scale_v, (CLASSES, cells)))[:1]
    mass = jnp.where(source_valid, source_total * scale_u * row_totals, 0.0)
    mass_ref[...] = own_part(pick_m, jnp.broadcast_to(mass, (8, cells)), mine, tile)[:1]
    share = jnp.where(source_valid, 1.0 / row_totals, 0.0)

    f_copy = pltpu.make_async_remote_copy(
        src_ref=fout,
        dst_ref=fin,
        send_sem=f_send,
        recv_sem=f_recv,
        device_id=(jnp.maximum(pair_at - 1, 0), row_at, col_at),
        device_id_type=MESH,
    )

    @pl.when(is_last)
    def _():
        class_values = lax.broadcasted_iota(jnp.int32, (CLASSES, cells), 0).astype(jnp.float32)
        fin[...] = jnp.where((labels == class_values) & target_valid, 1.0, 0.0)

    @pl.when(not_last)
    def _():
        f_copy.wait_recv()

    fates = transported(fin[...] * scale_v) * share
    fout[...] = fates

    @pl.when(not_first)
    def _():
        f_copy.start()

    fates_ref[0] = own_part(pick_f, fates, mine, tile)

    @others
    def _(block):
        x_copy(block).wait_send()

    @pl.when(not_first)
    def _():
        for block in range(n_block):
            relay(block).wait_send()
        f_copy.wait_send()

    @pl.when(is_last)
    def _():
        @others
        def _(block):
            final_copy(block).wait_send()


def per_device_fused(coords, final_coords, growth, counts, labels):
    tile = coords.shape[2]
    n_pair = lax.axis_size("pair")
    n_row = lax.axis_size("row")
    n_col = lax.axis_size("col")
    n_block = n_row * n_col
    cells = n_block * tile
    vmem = pl.BlockSpec(memory_space=pltpu.VMEM)
    dma = pltpu.SemaphoreType.DMA
    return pl.pallas_call(
        functools.partial(fused, (n_pair, n_row, n_col, tile)),
        out_shape=(
            pltpu.VMEM((1, CLASSES, tile), jnp.float32),
            pltpu.VMEM((1, tile), jnp.float32),
        ),
        in_specs=[pl.BlockSpec(memory_space=pltpu.SMEM)] + [pl.BlockSpec(memory_space=pl.ANY)] * 4,
        out_specs=(vmem, vmem),
        scratch_shapes=[
            pltpu.VMEM((coords.shape[1], 1, tile), jnp.float32),
            pltpu.VMEM((coords.shape[1], tile), jnp.float32),
            pltpu.VMEM((1, tile), jnp.float32),
            pltpu.VMEM((1, tile), jnp.int32),
            dma((4,)),
            pltpu.VMEM((n_block, HALF, LANES), jnp.float32),
            pltpu.VMEM((n_block, HALF, LANES), jnp.float32),
            pltpu.VMEM((cells, cells), jnp.bfloat16),
            pltpu.VMEM((cells, cells), jnp.bfloat16),
            pltpu.VMEM((CLASSES, cells), jnp.float32),
            pltpu.VMEM((CLASSES, cells), jnp.float32),
            pltpu.VMEM((cells // LANES, CLASSES, LANES), jnp.float32),
            pltpu.VMEM((cells // LANES, 8, LANES), jnp.float32),
            dma((n_block,)),
            dma((n_block,)),
            dma((n_block,)),
            dma((n_block,)),
            dma((n_block,)),
            dma,
            dma,
        ],
        compiler_params=pltpu.CompilerParams(collective_id=0, has_side_effects=True),
    )(counts, jnp.transpose(coords, (1, 0, 2)), final_coords, growth, labels[None, :])


def solution(mesh):
    placed = (
        P("pair", None, ("row", "col")),
        P(None, ("row", "col")),
        P("pair", ("row", "col")),
        P(),
        P(("row", "col")),
    )
    out = (P("pair", None, ("row", "col")), P("pair", ("row", "col")))

    def whole(coords, final_coords, growth, counts, labels):
        cells = coords.shape[2]
        blocks = mesh.shape["row"] * mesh.shape["col"]
        fits = (
            2 * cells == LANES * blocks
            and blocks % 2 == 0
            and coords.shape[0] == mesh.shape["pair"]
            and HALF < coords.shape[1] < 2 * HALF - 1
            and 4 * cells * cells <= FUSED_BYTES
        )
        body = per_device_fused if fits else per_device
        return jax.shard_map(
            body, mesh=mesh, in_specs=placed, out_specs=out, check_vma=False
        )(coords, final_coords, growth, counts, labels)

    return whole
```

```python
import functools
import jax
import jax.numpy as jnp
from jax import lax
from jax.experimental import pallas as pl
from jax.experimental.pallas import tpu as pltpu
from jax.sharding import PartitionSpec as P

CLASSES = 16
FUSED_BYTES = 16 * 1024 * 1024


cost_scale = 1.0
source_power = 0.5
target_power = 50.0 / 51.0


def shifted_2(block, axis, distance):
    devices = range(lax.axis_size(axis))
    route = [(i - distance, i) for i in devices if i - distance in devices]
    return lax.ppermute(block, axis, route)


def kernel_tile(sources, targets):
    cross = lax.dot_general(
        sources,
        targets,
        (((0,), (0,)), ((), ())),
        precision=lax.Precision.HIGHEST,
        preferred_element_type=jnp.float32,
    )
    source_norms = jnp.sum(sources * sources, axis=0)
    target_norms = jnp.sum(targets * targets, axis=0)
    return jnp.exp(-(source_norms[:, None] + target_norms[None, :] - 2.0 * cross) / cost_scale)


def forward(kernel, weights):
    return lax.dot_general(
        weights,
        kernel,
        (((1,), (1,)), ((), ())),
        precision=lax.Precision.HIGHEST,
        preferred_element_type=jnp.float32,
    )


def backward(kernel, scales):
    return jnp.dot(
        scales, kernel, precision=lax.Precision.HIGHEST, preferred_element_type=jnp.float32
    )


def per_device(coords, final_coords, growth, counts, labels):
    tile = coords.shape[2]
    n_pair = lax.axis_size("pair")
    n_row = lax.axis_size("row")
    n_col = lax.axis_size("col")
    pair_at = lax.axis_index("pair")
    row_at = lax.axis_index("row")
    col_at = lax.axis_index("col")
    source_count = n_col * tile
    target_count = n_row * tile
    own_coords = coords[0]
    sources, source_growth = (
        lax.all_gather(own_coords, "col", axis=1, tiled=True),
        lax.all_gather(growth[0], "col", axis=0, tiled=True),
    )
    shifted = shifted_2(own_coords, "pair", -1)
    is_last = pair_at == n_pair - 1
    own_targets = jnp.where(is_last, final_coords, shifted)
    label_values = labels.astype(jnp.float32)
    position = lax.iota(jnp.int32, target_count)
    targets, target_labels = (
        lax.all_gather(own_targets, "row", axis=1, tiled=True),
        lax.all_gather(label_values, "row", axis=0, tiled=True),
    )
    target_index = position // tile * (n_col * tile) + col_at * tile + position % tile

    def hand_over(fates_now):
        incoming = shifted_2(fates_now, "pair", -1)
        return lax.all_gather(incoming, "row", axis=1, tiled=True)

    source_number = counts[pair_at]
    target_number = counts[pair_at + 1]
    source_total = source_number.astype(jnp.float32)
    target_total = target_number.astype(jnp.float32)
    source_index = row_at * source_count + lax.iota(jnp.int32, source_count)
    source_valid = source_index < source_number
    target_valid = target_index < target_number
    kernel = kernel_tile(sources, targets)
    start_terms = forward(kernel, target_valid.astype(jnp.float32)[None, :])[0]
    start_rows = lax.psum(start_terms, "col")
    source_mass = jnp.where(source_valid, source_growth / source_total, 0.0)
    scale_u = jnp.where(source_valid, jnp.power(source_mass / start_rows, source_power), 0.0)
    column_terms = backward(kernel, scale_u)
    column_totals = lax.psum(column_terms, "row")
    target_mass = target_valid.astype(jnp.float32) / target_total
    scale_v = jnp.where(target_valid, jnp.power(target_mass / column_totals, target_power), 0.0)
    own_offset = col_at * tile
    own_valid = lax.dynamic_slice_in_dim(source_valid, own_offset, tile, 0)
    own_scale = lax.dynamic_slice_in_dim(scale_u, own_offset, tile, 0)
    class_values = lax.iota(jnp.int32, CLASSES).astype(jnp.float32)
    label_table = jnp.where(
        (target_labels[None, :] == class_values[:, None]) & target_valid[None, :], 1.0, 0.0
    ).astype(jnp.float32)
    empty = jnp.zeros((CLASSES, tile), jnp.float32)
    final_terms = forward(kernel, scale_v[None, :])[0]
    final_rows = lax.psum(final_terms, "col")
    own_rows = lax.dynamic_slice_in_dim(final_rows, own_offset, tile, 0)
    safe_rows = jnp.where(own_valid, own_rows, 1.0)

    def advance(turn, fates_now):
        carried = jnp.where(is_last, label_table, hand_over(fates_now))
        terms = forward(kernel, carried * scale_v[None, :])
        sums = lax.psum_scatter(terms, "col", scatter_dimension=1, tiled=True)
        return jnp.where(own_valid[None, :], sums / safe_rows[None, :], 0.0)

    fates = lax.fori_loop(0, n_pair, advance, empty)
    mass = jnp.where(own_valid, source_total * own_scale * own_rows, 0.0)
    return (fates[None], mass[None])


LANES = 128
HALF = 16
BIG = 1e30
MESH = pl.DeviceIdType.MESH


def split3(a):
    first = a.astype(jnp.bfloat16)
    rest = a - first.astype(jnp.float32)
    second = rest.astype(jnp.bfloat16)
    third = (rest - second.astype(jnp.float32)).astype(jnp.bfloat16)
    return first, second, third


def split2(a):
    first = a.astype(jnp.bfloat16)
    return first, (a - first.astype(jnp.float32)).astype(jnp.bfloat16)


def dot(a, b, dims):
    return lax.dot_general(a, b, (dims, ((), ())), preferred_element_type=jnp.float32)


def packed(block, extra):
    low = block[:HALF]
    rest = block.shape[0] - HALF
    fill = jnp.zeros((HALF - rest - 1, block.shape[1]), jnp.float32)
    high = jnp.concatenate([block[HALF:], extra, fill], axis=0)
    return jnp.concatenate([low, high], axis=1)


def unpacked(ref):
    lows, highs = [], []
    lane = lax.broadcasted_iota(jnp.int32, (HALF, LANES), 1)
    for j in range(ref.shape[0] // 2):
        a, b = ref[2 * j], ref[2 * j + 1]
        swap_a, swap_b = pltpu.roll(a, LANES // 2, 1), pltpu.roll(b, LANES // 2, 1)
        lows.append(jnp.where(lane < LANES // 2, a, swap_b))
        highs.append(jnp.where(lane < LANES // 2, swap_a, b))
    low, high = jnp.concatenate(lows, axis=1), jnp.concatenate(highs, axis=1)
    return jnp.concatenate([low, high], axis=0)


def own_part(ref, value, mine, tile):
    for j in range(ref.shape[0]):
        ref[j] = value[:, j * LANES : (j + 1) * LANES]
    chunk = ref[mine // 2]
    return pltpu.roll(chunk, (mine % 2) * tile, 1)[:, :tile]


def fused(
    sizes,
    counts_ref,
    coords_in,
    final_in,
    growth_in,
    labels_in,
    out_ref,
    coords_ref,
    final_ref,
    growth_ref,
    labels_ref,
    in_sems,
    xg,
    yg,
    k1,
    k2,
    fin,
    fout,
    pick_f,
    pick_m,
    x_send,
    x_recv,
    y_send,
    y_recv,
    z_send,
    f_send,
    f_recv,
):
    n_pair, n_row, n_col, tile = sizes
    n_block = n_row * n_col
    cells = n_block * tile
    pca = coords_ref.shape[0]
    last = n_pair - 1
    pair_at = lax.axis_index("pair")
    row_at = lax.axis_index("row")
    col_at = lax.axis_index("col")
    mine = row_at * n_col + col_at
    is_last = pair_at == last
    not_last = pair_at < last
    not_first = pair_at > 0

    def others(act):
        for block in range(n_block):
            pl.when(mine != block)(functools.partial(act, block))

    barrier = pltpu.get_barrier_semaphore()

    @others
    def _(block):
        r, c = divmod(block, n_col)
        pl.semaphore_signal(barrier, inc=1, device_id=(pair_at, r, c), device_id_type=MESH)

    @pl.when(not_last)
    def _():
        pl.semaphore_signal(
            barrier, inc=1, device_id=(pair_at + 1, row_at, col_at), device_id_type=MESH
        )

    source_loads = (
        pltpu.make_async_copy(coords_in, coords_ref, in_sems.at[0]),
        pltpu.make_async_copy(growth_in, growth_ref, in_sems.at[1]),
    )
    target_loads = (
        pltpu.make_async_copy(final_in, final_ref, in_sems.at[2]),
        pltpu.make_async_copy(labels_in, labels_ref, in_sems.at[3]),
    )
    for load in source_loads + target_loads:
        load.start()
    for load in source_loads + target_loads:
        load.wait()
    xg[mine] = packed(coords_ref[:, 0, :], growth_ref[...])

    @pl.when(is_last)
    def _():
        yg[mine] = packed(final_ref[...], labels_ref[...].astype(jnp.float32))

    @pl.when(not_first)
    def _():
        pl.semaphore_wait(barrier, n_block)

    @pl.when(pair_at == 0)
    def _():
        pl.semaphore_wait(barrier, n_block - 1)

    def x_copy(block):
        r, c = divmod(block, n_col)
        return pltpu.make_async_remote_copy(
            src_ref=xg.at[mine],
            dst_ref=xg.at[mine],
            send_sem=x_send.at[block],
            recv_sem=x_recv.at[mine],
            device_id=(pair_at, r, c),
            device_id_type=MESH,
        )

    def final_copy(block):
        r, c = divmod(block, n_col)
        return pltpu.make_async_remote_copy(
            src_ref=yg.at[mine],
            dst_ref=yg.at[mine],
            send_sem=z_send.at[block],
            recv_sem=y_recv.at[mine],
            device_id=(pair_at, r, c),
            device_id_type=MESH,
        )

    def relay(block):
        return pltpu.make_async_remote_copy(
            src_ref=xg.at[block],
            dst_ref=yg.at[block],
            send_sem=y_send.at[block],
            recv_sem=y_recv.at[block],
            device_id=(jnp.maximum(pair_at - 1, 0), row_at, col_at),
            device_id_type=MESH,
        )

    def arrival(buffer, sems, other):
        return pltpu.make_async_remote_copy(
            src_ref=buffer.at[other],
            dst_ref=buffer.at[other],
            send_sem=x_send.at[0],
            recv_sem=sems.at[other],
            device_id=(pair_at, row_at, col_at),
            device_id_type=MESH,
        )

    @others
    def _(block):
        x_copy(block).start()

        @pl.when(is_last)
        def _():
            final_copy(block).start()

    for block in range(n_block):

        @pl.when(mine != block)
        def _(block=block):
            arrival(xg, x_recv, block).wait_recv()

        @pl.when(not_first)
        def _(block=block):
            relay(block).start()

    for block in range(n_block):

        @pl.when(not_last | (mine != block))
        def _(block=block):
            arrival(yg, y_recv, block).wait_recv()

    source_number = counts_ref[pair_at]
    target_number = counts_ref[pair_at + 1]
    source_total = source_number.astype(jnp.float32)
    target_total = target_number.astype(jnp.float32)
    index = lax.broadcasted_iota(jnp.int32, (1, cells), 1)
    source_valid = index < source_number
    target_valid = index < target_number

    x = unpacked(xg)
    y = unpacked(yg)
    growth = x[pca : pca + 1]
    labels = y[pca : pca + 1]
    feature = lax.broadcasted_iota(jnp.int32, x.shape, 0)
    x = jnp.where(feature < pca, x, 0.0)
    y = jnp.where(feature < pca, y, 0.0)
    x_norm = jnp.sum(x * x, axis=0, keepdims=True)
    y_norm = jnp.where(target_valid, jnp.sum(y * y, axis=0, keepdims=True), BIG)
    a = jnp.where(feature < pca, x + x, jnp.where(feature == pca, -x_norm, 1.0))
    b = jnp.where(feature < pca, y, jnp.where(feature == pca, 1.0, -y_norm))
    a1, a2, a3 = split3(a)
    b1, b2, b3 = split3(b)
    left = jnp.concatenate([b1, b1, b2, b2, b1, b3], axis=0)
    right = jnp.concatenate([a1, a2, a1, a2, a3, a1], axis=0)
    totals = jnp.zeros((1, cells), jnp.float32)
    for j in range(cells // LANES):
        rows = slice(j * LANES, (j + 1) * LANES)
        values = jnp.exp(dot(left[:, rows], right, ((0,), (0,))))
        totals = totals + jnp.sum(values, axis=0, keepdims=True)
        high, low = split2(values)
        k1[rows, :] = high
        k2[rows, :] = low
    scale_u = jnp.where(source_valid, jnp.sqrt(growth / source_total / totals), 0.0)
    u1, u2 = split2(jnp.broadcast_to(scale_u, (HALF, cells)))
    u12 = jnp.concatenate([u1, u2], axis=0)
    column = dot(u12, k1[...], ((1,), (1,)))
    column_low = dot(u1, k2[...], ((1,), (1,)))
    column = column[:1] + column[HALF : HALF + 1] + column_low[:1]
    ratio = 1.0 / target_total / jnp.where(target_valid, column, 1.0)
    scale_v = jnp.where(target_valid, jnp.exp(target_power * jnp.log(ratio)), 0.0)

    def transported(weights):
        rows = weights.shape[0]
        w1, w2 = split2(weights)
        both = dot(jnp.concatenate([w1, w2], axis=0), k1[...], ((1,), (0,)))
        return both[:rows] + both[rows:] + dot(w1, k2[...], ((1,), (0,)))

    class_values = lax.broadcasted_iota(jnp.int32, (CLASSES, cells), 0).astype(jnp.float32)
    table = jnp.where((labels == class_values) & target_valid, 1.0, 0.0)
    spread_v = jnp.broadcast_to(scale_v, (CLASSES, cells))
    sums = transported(jnp.concatenate([table * scale_v, spread_v], axis=0))
    row_totals = sums[CLASSES : CLASSES + 1]
    share = jnp.where(source_valid, 1.0 / row_totals, 0.0)

    f_copy = pltpu.make_async_remote_copy(
        src_ref=fout,
        dst_ref=fin,
        send_sem=f_send,
        recv_sem=f_recv,
        device_id=(jnp.maximum(pair_at - 1, 0), row_at, col_at),
        device_id_type=MESH,
    )

    fout[...] = sums[:CLASSES] * share

    @pl.when(is_last & not_first)
    def _():
        f_copy.start()

    mass = jnp.where(source_valid, source_total * scale_u * row_totals, 0.0)
    out_ref[CLASSES:] = own_part(pick_m, jnp.broadcast_to(mass, (8, cells)), mine, tile)

    @pl.when(not_last)
    def _():
        f_copy.wait_recv()
        fout[...] = transported(fin[...] * scale_v) * share

    @pl.when(not_last & not_first)
    def _():
        f_copy.start()

    out_ref[:CLASSES] = own_part(pick_f, fout[...], mine, tile)

    @others
    def _(block):
        x_copy(block).wait_send()

    @pl.when(not_first)
    def _():
        for block in range(n_block):
            relay(block).wait_send()
        f_copy.wait_send()

    @pl.when(is_last)
    def _():
        @others
        def _(block):
            final_copy(block).wait_send()


def per_device_fused(coords, final_coords, growth, counts, labels):
    tile = coords.shape[2]
    n_pair = lax.axis_size("pair")
    n_row = lax.axis_size("row")
    n_col = lax.axis_size("col")
    n_block = n_row * n_col
    cells = n_block * tile
    vmem = pl.BlockSpec(memory_space=pltpu.VMEM)
    dma = pltpu.SemaphoreType.DMA
    result = pl.pallas_call(
        functools.partial(fused, (n_pair, n_row, n_col, tile)),
        out_shape=pltpu.VMEM((CLASSES + 8, tile), jnp.float32),
        in_specs=[pl.BlockSpec(memory_space=pltpu.SMEM)] + [pl.BlockSpec(memory_space=pl.ANY)] * 4,
        out_specs=vmem,
        scratch_shapes=[
            pltpu.VMEM((coords.shape[1], 1, tile), jnp.float32),
            pltpu.VMEM((coords.shape[1], tile), jnp.float32),
            pltpu.VMEM((1, tile), jnp.float32),
            pltpu.VMEM((1, tile), jnp.int32),
            dma((4,)),
            pltpu.VMEM((n_block, HALF, LANES), jnp.float32),
            pltpu.VMEM((n_block, HALF, LANES), jnp.float32),
            pltpu.VMEM((cells, cells), jnp.bfloat16),
            pltpu.VMEM((cells, cells), jnp.bfloat16),
            pltpu.VMEM((CLASSES, cells), jnp.float32),
            pltpu.VMEM((CLASSES, cells), jnp.float32),
            pltpu.VMEM((cells // LANES, CLASSES, LANES), jnp.float32),
            pltpu.VMEM((cells // LANES, 8, LANES), jnp.float32),
            dma((n_block,)),
            dma((n_block,)),
            dma((n_block,)),
            dma((n_block,)),
            dma((n_block,)),
            dma,
            dma,
        ],
        compiler_params=pltpu.CompilerParams(collective_id=0, has_side_effects=True),
    )(counts, jnp.transpose(coords, (1, 0, 2)), final_coords, growth, labels[None, :])
    return result[None, :CLASSES], result[CLASSES : CLASSES + 1]


def solution(mesh):
    placed = (
        P("pair", None, ("row", "col")),
        P(None, ("row", "col")),
        P("pair", ("row", "col")),
        P(),
        P(("row", "col")),
    )
    out = (P("pair", None, ("row", "col")), P("pair", ("row", "col")))

    def whole(coords, final_coords, growth, counts, labels):
        cells = coords.shape[2]
        blocks = mesh.shape["row"] * mesh.shape["col"]
        fits = (
            2 * cells == LANES * blocks
            and blocks % 2 == 0
            and coords.shape[0] == mesh.shape["pair"]
            and HALF < coords.shape[1] < 2 * HALF - 1
            and 4 * cells * cells <= FUSED_BYTES
        )
        body = per_device_fused if fits else per_device
        return jax.shard_map(
            body, mesh=mesh, in_specs=placed, out_specs=out, check_vma=False
        )(coords, final_coords, growth, counts, labels)

    return whole
```

```python
import functools
import jax
import jax.numpy as jnp
from jax import lax
from jax.experimental import pallas as pl
from jax.experimental.pallas import tpu as pltpu
from jax.sharding import PartitionSpec as P

CLASSES = 16
FUSED_BYTES = 16 * 1024 * 1024


cost_scale = 1.0
source_power = 0.5
target_power = 50.0 / 51.0


def shifted_2(block, axis, distance):
    devices = range(lax.axis_size(axis))
    route = [(i - distance, i) for i in devices if i - distance in devices]
    return lax.ppermute(block, axis, route)


def kernel_tile(sources, targets):
    cross = lax.dot_general(
        sources,
        targets,
        (((0,), (0,)), ((), ())),
        precision=lax.Precision.HIGHEST,
        preferred_element_type=jnp.float32,
    )
    source_norms = jnp.sum(sources * sources, axis=0)
    target_norms = jnp.sum(targets * targets, axis=0)
    return jnp.exp(-(source_norms[:, None] + target_norms[None, :] - 2.0 * cross) / cost_scale)


def forward(kernel, weights):
    return lax.dot_general(
        weights,
        kernel,
        (((1,), (1,)), ((), ())),
        precision=lax.Precision.HIGHEST,
        preferred_element_type=jnp.float32,
    )


def backward(kernel, scales):
    return jnp.dot(
        scales, kernel, precision=lax.Precision.HIGHEST, preferred_element_type=jnp.float32
    )


def per_device(coords, final_coords, growth, counts, labels):
    tile = coords.shape[2]
    n_pair = lax.axis_size("pair")
    n_row = lax.axis_size("row")
    n_col = lax.axis_size("col")
    pair_at = lax.axis_index("pair")
    row_at = lax.axis_index("row")
    col_at = lax.axis_index("col")
    source_count = n_col * tile
    target_count = n_row * tile
    own_coords = coords[0]
    sources, source_growth = (
        lax.all_gather(own_coords, "col", axis=1, tiled=True),
        lax.all_gather(growth[0], "col", axis=0, tiled=True),
    )
    shifted = shifted_2(own_coords, "pair", -1)
    is_last = pair_at == n_pair - 1
    own_targets = jnp.where(is_last, final_coords, shifted)
    label_values = labels.astype(jnp.float32)
    position = lax.iota(jnp.int32, target_count)
    targets, target_labels = (
        lax.all_gather(own_targets, "row", axis=1, tiled=True),
        lax.all_gather(label_values, "row", axis=0, tiled=True),
    )
    target_index = position // tile * (n_col * tile) + col_at * tile + position % tile

    def hand_over(fates_now):
        incoming = shifted_2(fates_now, "pair", -1)
        return lax.all_gather(incoming, "row", axis=1, tiled=True)

    source_number = counts[pair_at]
    target_number = counts[pair_at + 1]
    source_total = source_number.astype(jnp.float32)
    target_total = target_number.astype(jnp.float32)
    source_index = row_at * source_count + lax.iota(jnp.int32, source_count)
    source_valid = source_index < source_number
    target_valid = target_index < target_number
    kernel = kernel_tile(sources, targets)
    start_terms = forward(kernel, target_valid.astype(jnp.float32)[None, :])[0]
    start_rows = lax.psum(start_terms, "col")
    source_mass = jnp.where(source_valid, source_growth / source_total, 0.0)
    scale_u = jnp.where(source_valid, jnp.power(source_mass / start_rows, source_power), 0.0)
    column_terms = backward(kernel, scale_u)
    column_totals = lax.psum(column_terms, "row")
    target_mass = target_valid.astype(jnp.float32) / target_total
    scale_v = jnp.where(target_valid, jnp.power(target_mass / column_totals, target_power), 0.0)
    own_offset = col_at * tile
    own_valid = lax.dynamic_slice_in_dim(source_valid, own_offset, tile, 0)
    own_scale = lax.dynamic_slice_in_dim(scale_u, own_offset, tile, 0)
    class_values = lax.iota(jnp.int32, CLASSES).astype(jnp.float32)
    label_table = jnp.where(
        (target_labels[None, :] == class_values[:, None]) & target_valid[None, :], 1.0, 0.0
    ).astype(jnp.float32)
    empty = jnp.zeros((CLASSES, tile), jnp.float32)
    final_terms = forward(kernel, scale_v[None, :])[0]
    final_rows = lax.psum(final_terms, "col")
    own_rows = lax.dynamic_slice_in_dim(final_rows, own_offset, tile, 0)
    safe_rows = jnp.where(own_valid, own_rows, 1.0)

    def advance(turn, fates_now):
        carried = jnp.where(is_last, label_table, hand_over(fates_now))
        terms = forward(kernel, carried * scale_v[None, :])
        sums = lax.psum_scatter(terms, "col", scatter_dimension=1, tiled=True)
        return jnp.where(own_valid[None, :], sums / safe_rows[None, :], 0.0)

    fates = lax.fori_loop(0, n_pair, advance, empty)
    mass = jnp.where(own_valid, source_total * own_scale * own_rows, 0.0)
    return (fates[None], mass[None])


LANES = 128
HALF = 16
BIG = 1e30
LIFT = 2.0**57
MESH = pl.DeviceIdType.MESH


def split3(a):
    first = a.astype(jnp.bfloat16)
    rest = a - first.astype(jnp.float32)
    second = rest.astype(jnp.bfloat16)
    third = (rest - second.astype(jnp.float32)).astype(jnp.bfloat16)
    return first, second, third


def split2(a):
    first = a.astype(jnp.bfloat16)
    return first, (a - first.astype(jnp.float32)).astype(jnp.bfloat16)


def dot(a, b, dims):
    return lax.dot_general(a, b, (dims, ((), ())), preferred_element_type=jnp.float32)


def packed(block, extra):
    low = block[:HALF]
    rest = block.shape[0] - HALF
    fill = jnp.zeros((HALF - rest - 1, block.shape[1]), jnp.float32)
    high = jnp.concatenate([block[HALF:], extra, fill], axis=0)
    return jnp.concatenate([low, high], axis=1)


def unpacked(ref):
    lows, highs = [], []
    lane = lax.broadcasted_iota(jnp.int32, (HALF, LANES), 1)
    for j in range(ref.shape[0] // 2):
        a, b = ref[2 * j], ref[2 * j + 1]
        swap_a, swap_b = pltpu.roll(a, LANES // 2, 1), pltpu.roll(b, LANES // 2, 1)
        lows.append(jnp.where(lane < LANES // 2, a, swap_b))
        highs.append(jnp.where(lane < LANES // 2, swap_a, b))
    low, high = jnp.concatenate(lows, axis=1), jnp.concatenate(highs, axis=1)
    return jnp.concatenate([low, high], axis=0)


def own_part(ref, value, mine, tile):
    for j in range(ref.shape[0]):
        ref[j] = value[:, j * LANES : (j + 1) * LANES]
    chunk = ref[mine // 2]
    return pltpu.roll(chunk, (mine % 2) * tile, 1)[:, :tile]


def fused(
    sizes,
    counts_ref,
    coords_in,
    final_in,
    growth_in,
    labels_in,
    fates_ref,
    mass_ref,
    coords_ref,
    final_ref,
    growth_ref,
    labels_ref,
    in_sems,
    xg,
    yg,
    k1,
    k2,
    fin,
    fout,
    pick_f,
    pick_m,
    x_send,
    x_recv,
    y_send,
    y_recv,
    z_send,
    f_send,
    f_recv,
):
    n_pair, n_row, n_col, tile = sizes
    n_block = n_row * n_col
    cells = n_block * tile
    pca = coords_ref.shape[0]
    last = n_pair - 1
    pair_at = lax.axis_index("pair")
    row_at = lax.axis_index("row")
    col_at = lax.axis_index("col")
    mine = row_at * n_col + col_at
    is_last = pair_at == last
    not_last = pair_at < last
    not_first = pair_at > 0

    def others(act):
        for block in range(n_block):
            pl.when(mine != block)(functools.partial(act, block))

    barrier = pltpu.get_barrier_semaphore()

    @others
    def _(block):
        r, c = divmod(block, n_col)
        pl.semaphore_signal(barrier, inc=1, device_id=(pair_at, r, c), device_id_type=MESH)

    @pl.when(not_last)
    def _():
        pl.semaphore_signal(
            barrier, inc=1, device_id=(pair_at + 1, row_at, col_at), device_id_type=MESH
        )

    source_loads = (
        pltpu.make_async_copy(coords_in, coords_ref, in_sems.at[0]),
        pltpu.make_async_copy(growth_in, growth_ref, in_sems.at[1]),
    )
    target_loads = (
        pltpu.make_async_copy(final_in, final_ref, in_sems.at[2]),
        pltpu.make_async_copy(labels_in, labels_ref, in_sems.at[3]),
    )
    for load in source_loads + target_loads:
        load.start()
    for load in source_loads + target_loads:
        load.wait()
    xg[mine] = packed(coords_ref[:, 0, :], growth_ref[...])

    @pl.when(is_last)
    def _():
        yg[mine] = packed(final_ref[...], labels_ref[...].astype(jnp.float32))

    @pl.when(not_first)
    def _():
        pl.semaphore_wait(barrier, n_block)

    @pl.when(pair_at == 0)
    def _():
        pl.semaphore_wait(barrier, n_block - 1)

    def x_copy(block):
        r, c = divmod(block, n_col)
        return pltpu.make_async_remote_copy(
            src_ref=xg.at[mine],
            dst_ref=xg.at[mine],
            send_sem=x_send.at[block],
            recv_sem=x_recv.at[mine],
            device_id=(pair_at, r, c),
            device_id_type=MESH,
        )

    def final_copy(block):
        r, c = divmod(block, n_col)
        return pltpu.make_async_remote_copy(
            src_ref=yg.at[mine],
            dst_ref=yg.at[mine],
            send_sem=z_send.at[block],
            recv_sem=y_recv.at[mine],
            device_id=(pair_at, r, c),
            device_id_type=MESH,
        )

    def relay(block):
        return pltpu.make_async_remote_copy(
            src_ref=xg.at[block],
            dst_ref=yg.at[block],
            send_sem=y_send.at[block],
            recv_sem=y_recv.at[block],
            device_id=(jnp.maximum(pair_at - 1, 0), row_at, col_at),
            device_id_type=MESH,
        )

    def arrival(buffer, sems, other):
        return pltpu.make_async_remote_copy(
            src_ref=buffer.at[other],
            dst_ref=buffer.at[other],
            send_sem=x_send.at[0],
            recv_sem=sems.at[other],
            device_id=(pair_at, row_at, col_at),
            device_id_type=MESH,
        )

    @others
    def _(block):
        x_copy(block).start()

        @pl.when(is_last)
        def _():
            final_copy(block).start()

    for block in range(n_block):

        @pl.when(mine != block)
        def _(block=block):
            arrival(xg, x_recv, block).wait_recv()

        @pl.when(not_first)
        def _(block=block):
            relay(block).start()

    for block in range(n_block):

        @pl.when(not_last | (mine != block))
        def _(block=block):
            arrival(yg, y_recv, block).wait_recv()

    source_number = counts_ref[pair_at]
    target_number = counts_ref[pair_at + 1]
    source_total = source_number.astype(jnp.float32)
    target_total = target_number.astype(jnp.float32)
    index = lax.broadcasted_iota(jnp.int32, (1, cells), 1)
    source_valid = index < source_number
    target_valid = index < target_number

    x = unpacked(xg)
    y = unpacked(yg)
    growth = x[pca : pca + 1]
    labels = y[pca : pca + 1]
    feature = lax.broadcasted_iota(jnp.int32, x.shape, 0)
    x = jnp.where(feature < pca, x, 0.0)
    y = jnp.where(feature < pca, y, 0.0)
    x_norm = jnp.sum(x * x, axis=0, keepdims=True)
    y_norm = jnp.where(target_valid, jnp.sum(y * y, axis=0, keepdims=True), BIG)
    a = jnp.where(feature < pca, x + x, jnp.where(feature == pca, -x_norm, 1.0))
    b = jnp.where(feature < pca, y, jnp.where(feature == pca, 1.0, -y_norm))
    a1, a2, a3 = split3(a)
    b1, b2, b3 = split3(b)
    left = jnp.concatenate([b1, b1, b2, b2, b1, b3], axis=0)
    right = jnp.concatenate([a1, a2, a1, a2, a3, a1], axis=0)
    totals = jnp.zeros((1, cells), jnp.float32)
    for j in range(cells // LANES):
        rows = slice(j * LANES, (j + 1) * LANES)
        values = jnp.exp(dot(left[:, rows], right, ((0,), (0,))))
        totals = totals + jnp.sum(values, axis=0, keepdims=True)
        high, low = split2(values * LIFT)
        k1[rows, :] = high
        k2[rows, :] = low
    scale_u = jnp.where(source_valid, jnp.sqrt(growth / source_total / totals), 0.0)
    u1, u2 = split2(jnp.broadcast_to(scale_u, (HALF, cells)))
    u12 = jnp.concatenate([u1, u2], axis=0)
    column = dot(u12, k1[...], ((1,), (1,)))
    column_low = dot(u1, k2[...], ((1,), (1,)))
    column = (column[:1] + column[HALF : HALF + 1] + column_low[:1]) * (1.0 / LIFT)
    ratio = 1.0 / target_total / jnp.where(target_valid, column, 1.0)
    scale_v = jnp.where(target_valid, jnp.exp(target_power * jnp.log(ratio)), 0.0)

    def transported(weights):
        w1, w2 = split2(weights)
        both = dot(jnp.concatenate([w1, w2], axis=0), k1[...], ((1,), (0,)))
        return (both[:CLASSES] + both[CLASSES:] + dot(w1, k2[...], ((1,), (0,)))) * (1.0 / LIFT)

    row_totals = transported(jnp.broadcast_to(scale_v, (CLASSES, cells)))[:1]
    mass = jnp.where(source_valid, source_total * scale_u * row_totals, 0.0)
    mass_ref[...] = own_part(pick_m, jnp.broadcast_to(mass, (8, cells)), mine, tile)[:1]
    share = jnp.where(source_valid, 1.0 / row_totals, 0.0)

    f_copy = pltpu.make_async_remote_copy(
        src_ref=fout,
        dst_ref=fin,
        send_sem=f_send,
        recv_sem=f_recv,
        device_id=(jnp.maximum(pair_at - 1, 0), row_at, col_at),
        device_id_type=MESH,
    )

    @pl.when(is_last)
    def _():
        class_values = lax.broadcasted_iota(jnp.int32, (CLASSES, cells), 0).astype(jnp.float32)
        fin[...] = jnp.where((labels == class_values) & target_valid, 1.0, 0.0)

    @pl.when(not_last)
    def _():
        f_copy.wait_recv()

    fates = transported(fin[...] * scale_v) * share
    fout[...] = fates

    @pl.when(not_first)
    def _():
        f_copy.start()

    fates_ref[0] = own_part(pick_f, fates, mine, tile)

    @others
    def _(block):
        x_copy(block).wait_send()

    @pl.when(not_first)
    def _():
        for block in range(n_block):
            relay(block).wait_send()
        f_copy.wait_send()

    @pl.when(is_last)
    def _():
        @others
        def _(block):
            final_copy(block).wait_send()


def per_device_fused(coords, final_coords, growth, counts, labels):
    tile = coords.shape[2]
    n_pair = lax.axis_size("pair")
    n_row = lax.axis_size("row")
    n_col = lax.axis_size("col")
    n_block = n_row * n_col
    cells = n_block * tile
    vmem = pl.BlockSpec(memory_space=pltpu.VMEM)
    dma = pltpu.SemaphoreType.DMA
    return pl.pallas_call(
        functools.partial(fused, (n_pair, n_row, n_col, tile)),
        out_shape=(
            pltpu.VMEM((1, CLASSES, tile), jnp.float32),
            pltpu.VMEM((1, tile), jnp.float32),
        ),
        in_specs=[pl.BlockSpec(memory_space=pltpu.SMEM)] + [pl.BlockSpec(memory_space=pl.ANY)] * 4,
        out_specs=(vmem, vmem),
        scratch_shapes=[
            pltpu.VMEM((coords.shape[1], 1, tile), jnp.float32),
            pltpu.VMEM((coords.shape[1], tile), jnp.float32),
            pltpu.VMEM((1, tile), jnp.float32),
            pltpu.VMEM((1, tile), jnp.int32),
            dma((4,)),
            pltpu.VMEM((n_block, HALF, LANES), jnp.float32),
            pltpu.VMEM((n_block, HALF, LANES), jnp.float32),
            pltpu.VMEM((cells, cells), jnp.bfloat16),
            pltpu.VMEM((cells, cells), jnp.bfloat16),
            pltpu.VMEM((CLASSES, cells), jnp.float32),
            pltpu.VMEM((CLASSES, cells), jnp.float32),
            pltpu.VMEM((cells // LANES, CLASSES, LANES), jnp.float32),
            pltpu.VMEM((cells // LANES, 8, LANES), jnp.float32),
            dma((n_block,)),
            dma((n_block,)),
            dma((n_block,)),
            dma((n_block,)),
            dma((n_block,)),
            dma,
            dma,
        ],
        compiler_params=pltpu.CompilerParams(collective_id=0, has_side_effects=True),
    )(counts, jnp.transpose(coords, (1, 0, 2)), final_coords, growth, labels[None, :])


def solution(mesh):
    placed = (
        P("pair", None, ("row", "col")),
        P(None, ("row", "col")),
        P("pair", ("row", "col")),
        P(),
        P(("row", "col")),
    )
    out = (P("pair", None, ("row", "col")), P("pair", ("row", "col")))

    def whole(coords, final_coords, growth, counts, labels):
        cells = coords.shape[2]
        blocks = mesh.shape["row"] * mesh.shape["col"]
        fits = (
            2 * cells == LANES * blocks
            and blocks % 2 == 0
            and coords.shape[0] == mesh.shape["pair"]
            and HALF < coords.shape[1] < 2 * HALF - 1
            and 4 * cells * cells <= FUSED_BYTES
        )
        body = per_device_fused if fits else per_device
        return jax.shard_map(
            body, mesh=mesh, in_specs=placed, out_specs=out, check_vma=False
        )(coords, final_coords, growth, counts, labels)

    return whole
```
